32 devices in a mesh: loop: 8 (over y, x, core), dp: 4 (over z).
Axes of the slice: x: 2, y: 2, z: 4, core: 2. Of those that a mesh axis runs over, the one named last changes fastest.
Arguments:
- codes: bfloat16 [2048, 16, 1024], P(('loop', 'dp')), may hold values from -64 to 64, as said below
- cand_hidden: bfloat16 [2048, 1024], P(('loop', 'dp')), may hold values from -5 to 5, as said below
- proj: bfloat16 [1024, 1024], replicated, may hold values from -1 to 2, as said below
- gold: int32 [2048], P(('loop', 'dp')), may hold values from 0 to 511
Outputs:
- context_loss: float32 [2048], P(('loop', 'dp'))
- code_grad: float32 [2048, 16, 1024], P(('loop', 'dp'))
- proj_grad: float32 [1024, 1024], P(('loop', 'dp'))
The draws below stay inside these ranges and needn't reach their ends.
Inputs may be any that keep to these rules, and one draw needn't show every extreme that they name: codes stay within this range. `cand_hidden`: CLS states stay within this range. `proj`: projection entries stay within this range.
All inputs are finite; a program needn't handle non-finite values.
Results may differ from the reference program's by a relative error of at most 0.0085.
Values may be sent and summed in bfloat16 or wider, within the bound.
A program may use at most 128 MiB of HBM per device.

```python
import math
import jax
import jax.numpy as jnp
from jax import lax

D = 1024
M = 16
B = 64
CONTEXTS = 2048
N_LOOP = 8
N_DP = 4


def base_hidden(key):
    return jnp.clip(jax.random.normal(jax.random.fold_in(key, 7), (CONTEXTS, D), jnp.float32), -5.0, 5.0)


def draw_cand_hidden(key, part):
    return base_hidden(key).astype(jnp.bfloat16)


def draw_proj(key, part):
    noise = jnp.clip(jax.random.normal(jax.random.fold_in(key, 13), (D, D), jnp.float32), -6.0, 6.0)
    matrix = noise / math.sqrt(D)
    return matrix.astype(jnp.bfloat16)


def draw_codes(key, part):
    rough = jnp.clip(jax.random.normal(jax.random.fold_in(key, 21), (CONTEXTS, M, D), jnp.float32), -4.0, 4.0) * 4.0
    return rough.astype(jnp.bfloat16)


def set_ends(drawn, rng, low, top_value):
    place = [jax.random.randint(jax.random.fold_in(rng, axis), (), 0, length) for axis, length in enumerate(drawn.shape)]
    main_axis = drawn.shape.index(max(drawn.shape))
    neighbour = place[:main_axis] + [(place[main_axis] + 1) % drawn.shape[main_axis]] + place[main_axis + 1:]
    return drawn.at[tuple(place)].set(low).at[tuple(neighbour)].set(top_value)


def setup_inputs(seed: int = 0) -> dict:
    arg_keys = jax.random.split(jax.random.key(seed), 5)
    return {
        "codes": draw_codes(jax.random.fold_in(arg_keys[4], 71), 0),
        "cand_hidden": draw_cand_hidden(jax.random.fold_in(arg_keys[4], 71), 0),
        "proj": draw_proj(jax.random.fold_in(arg_keys[4], 71), 0),
        "gold": set_ends(jax.random.randint(arg_keys[3], (CONTEXTS,), 0, B * N_LOOP), jax.random.fold_in(arg_keys[3], 1), 0, (B * N_LOOP) - 1).astype(jnp.int32),
    }


def regroup(array):
    shape = array.shape[1:]
    split = array.reshape((N_LOOP, N_DP, B) + shape)
    moved = jnp.swapaxes(split, 0, 1)
    return moved.reshape((N_DP, N_LOOP * B) + shape)


def ungroup(array):
    shape = array.shape[2:]
    split = array.reshape((N_DP, N_LOOP, B) + shape)
    moved = jnp.swapaxes(split, 0, 1)
    return moved.reshape((N_LOOP * N_DP * B,) + shape)


def reference(codes, cand_hidden, proj, gold):
    inv_scale = D ** -0.5

    def one_group(inputs):
        group_codes, group_hidden, group_gold = inputs
        count = group_hidden.shape[0]
        cand_embed = jnp.dot(group_hidden, proj, preferred_element_type=jnp.float32).astype(jnp.bfloat16)
        code_rows = group_codes.reshape(count * M, D)
        raw = lax.dot_general(cand_embed, code_rows, (((1,), (1,)), ((), ())), preferred_element_type=jnp.float32)
        logits = raw.reshape(count, count, M) * inv_scale
        top_logit = jnp.max(logits, axis=-1, keepdims=True)
        weights = jnp.exp(logits - top_logit)
        probs = weights / jnp.sum(weights, axis=-1, keepdims=True)
        scores = jnp.sum(probs * logits, axis=-1)
        top_score = jnp.max(scores, axis=0)
        log_total = top_score + jnp.log(jnp.sum(jnp.exp(scores - top_score[None, :]), axis=0))
        cand_ids = jnp.arange(count, dtype=jnp.int32)
        gold_hot = (cand_ids[:, None] == group_gold[None, :]).astype(jnp.float32)
        context_loss = log_total - jnp.sum(gold_hot * scores, axis=0)
        score_grad = jnp.exp(scores - log_total[None, :]) - gold_hot
        logit_grad = (score_grad[:, :, None] * probs * (1.0 + logits - scores[:, :, None]) * inv_scale).astype(jnp.bfloat16)
        logit_grad = logit_grad.reshape(count, count * M)
        code_grad = lax.dot_general(logit_grad, cand_embed, (((0,), (0,)), ((), ())), preferred_element_type=jnp.float32)
        embed_grad = jnp.dot(logit_grad, code_rows, preferred_element_type=jnp.float32).astype(jnp.bfloat16)
        proj_part = lax.dot_general(group_hidden, embed_grad, (((0,), (0,)), ((), ())), preferred_element_type=jnp.float32)
        return context_loss, code_grad.reshape(count, M, D), proj_part

    losses, code_grads, proj_parts = lax.map(one_group, (regroup(codes), regroup(cand_hidden), regroup(gold)))
    return ungroup(losses), ungroup(code_grads), jnp.sum(proj_parts, axis=0)
```

```python
import functools

import jax
import jax.numpy as jnp
from jax import lax
from jax.experimental import pallas as pl
from jax.experimental.pallas import tpu as pltpu
from jax.sharding import PartitionSpec as P

MESH = pl.DeviceIdType.MESH
F32 = jnp.float32
BF16 = jnp.bfloat16
LANES = 128
STEP = 64
TILE = 256
LAG = 2
NT = (((1,), (1,)), ((), ()))


def dot(a, b):
    return jnp.dot(a, b, preferred_element_type=F32)


def body(
    ring, groups, ctx, per,
    codes_ref, hidden_ref, proj_ref, gold_ref,
    loss_ref, code_ref, proj_out,
    codes, proj, gold_v, perm, rows, held, embed, logits, slopes, scores, grads, gradt, hidt,
    e_own, e_sib, e_sum, e_via_x, e_via_y, e_x, e_y, e_fwd_x, e_fwd_y,
    p_own, p_in, q_own, q_in,
    local_sem, proj_sem,
    bx_send, bx_recv, by_send, by_recv, bdx_send, bdx_recv, bdy_send, bdy_recv,
    bs_send, bs_recv, h_send, h_recv, hs_send, hs_recv, es_send, es_recv,
    evx_send, evx_recv, evy_send, evy_recv, ex_send, ex_recv, ey_send, ey_recv,
    z_send, z_recv, q_send, q_recv,
):
    batch, width = hidden_ref.shape
    chips = ring // 2
    tall = chips // 2
    cands = ring * batch
    n_rows = ctx * per
    me = lax.axis_index("loop")
    group = lax.axis_index("dp")
    chip, par = me // 2, me % 2
    y, x = chip // 2, chip % 2
    inv_scale = width ** -0.5

    def device(yy, xx, pp):
        return (yy * 2 + xx) * 2 + pp

    sibling = device(y, x, 1 - par)
    across = device(y, 1 - x, par)
    mates = range(tall - 1)
    ups = [(y + 1 + k) % tall for k in mates]
    downs = [(y + tall - 1 - k) % tall for k in mates]

    barrier = pltpu.get_barrier_semaphore()
    for k in range(1, ring):
        pl.semaphore_signal(barrier, 1, device_id={"loop": (me + k) % ring}, device_id_type=MESH)
    for k in range(1, groups):
        pl.semaphore_signal(barrier, 1, device_id={"dp": (group + k) % groups}, device_id_type=MESH)

    get_hidden = pltpu.make_async_copy(hidden_ref, held.at[me], local_sem.at[0])
    get_hidden.start()
    get_proj = []
    for t in range(width // TILE):
        cols = slice(t * TILE, (t + 1) * TILE)
        copy = pltpu.make_async_copy(proj_ref.at[:, cols], proj.at[:, cols], proj_sem.at[t])
        copy.start()
        get_proj.append(copy)
    get_codes = pltpu.make_async_copy(codes_ref, codes, local_sem.at[1])
    get_codes.start()
    get_gold = pltpu.make_async_copy(gold_ref, gold_v, local_sem.at[2])
    get_gold.start()

    row_tile = 128

    def permutation(outer, inner):
        @pl.loop(0, n_rows // row_tile)
        def _(t):
            start = pl.multiple_of(t * row_tile, row_tile)
            r = lax.broadcasted_iota(jnp.int32, (row_tile, n_rows), 0) + start
            c = lax.broadcasted_iota(jnp.int32, (row_tile, n_rows), 1)
            perm[pl.ds(start, row_tile), :] = jnp.where(
                c == (r % inner) * outer + r // inner, 1.0, 0.0).astype(BF16)

    permutation(per, ctx)

    def send(src, dst, ssem, rsem, where):
        copy = pltpu.make_async_remote_copy(
            src_ref=src, dst_ref=dst, send_sem=ssem, recv_sem=rsem,
            device_id=where, device_id_type=MESH)
        copy.start()
        return copy

    def spot_of(owner):
        return pl.ds(pl.multiple_of(owner * batch, batch), batch)

    piece = batch // 2

    def piece_of(owner, part):
        return embed.at[pl.ds(pl.multiple_of(owner * batch + part * piece, piece), piece)]

    get_hidden.wait()
    for t in range(width // TILE):
        cols = slice(t * TILE, (t + 1) * TILE)
        get_proj[t].wait()
        embed[spot_of(me), cols] = dot(held[me], proj[:, cols]).astype(BF16)
    pl.semaphore_wait(barrier, ring + groups - 2)

    started = []

    def post(*args):
        copy = send(*args)
        started.append(copy)
        return copy

    def pass_on(slot, owner):
        block = embed.at[spot_of(owner)]
        return post(block, block, bs_send.at[slot], bs_recv.at[slot], {"loop": sibling})

    own = [piece_of(me, 0), piece_of(me, 1)]
    from_x, from_y = [None, None], [[None, None] for _ in mates]
    for first in range(2):
        from_x[first] = post(own[first], own[first], bx_send.at[first], bx_recv.at[first],
                             {"loop": across})
        for k in mates:
            last = 1 - first
            from_y[k][last] = post(own[last], own[last], by_send.at[k, last],
                                   by_recv.at[k, last], {"loop": device(ups[k], x, par)})
    shared = [pass_on(0, me)]

    get_codes.wait()

    @pl.loop(0, width // TILE)
    def _(t):
        cols = pl.ds(pl.multiple_of(t * TILE, TILE), TILE)
        rows[:, cols] = dot(perm[...], codes[:, cols]).astype(BF16)

    diag_y, diag_x = [], []
    from_x[0].wait_recv()
    for k in mates:
        block = piece_of(across, 0)
        diag_y.append(post(block, block, bdy_send.at[k], bdy_recv.at[k],
                           {"loop": device(ups[k], x, par)}))
    for k in mates:
        from_y[k][1].wait_recv()
        block = piece_of(device(downs[k], x, par), 1)
        diag_x.append(post(block, block, bdx_send.at[k], bdx_recv.at[k], {"loop": across}))

    far = []
    for k in range(chips - 1):
        to = (chip + 1 + k) % chips
        far.append(post(hidden_ref, held.at[me], h_send.at[k], h_recv.at[k],
                        {"loop": to * 2 + par}))
    near = [post(hidden_ref, held.at[me], hs_send.at[chips - 1], hs_recv.at[chips - 1],
                 {"loop": sibling})]

    def forward(owners):
        count = len(owners) * batch
        spots = [spot_of(o) for o in owners]

        @pl.loop(0, n_rows // TILE)
        def _(t):
            cols = pl.ds(pl.multiple_of(t * TILE, TILE), TILE)
            logits[:count, cols] = lax.dot_general(
                jnp.concatenate([embed[spot, :] for spot in spots], axis=0), rows[cols, :], NT,
                preferred_element_type=F32) * inv_scale

        step = STEP
        per_owner = batch // step

        for j, o in enumerate(owners):
            @pl.loop(0, per_owner)
            def _(t):
                src = pl.ds(pl.multiple_of(j * batch + t * step, step), step)
                at = pl.ds(pl.multiple_of(o * batch + t * step, step), step)
                parts = [logits[src, i * LANES:(i + 1) * LANES] for i in range(n_rows // LANES)]

                def over(values, op):
                    while len(values) > 1:
                        values = [op(*values[i:i + 2]) if i + 1 < len(values) else values[i]
                                  for i in range(0, len(values), 2)]
                    total = values[0]
                    shift = ctx
                    while shift < LANES:
                        total = op(total, pltpu.roll(total, shift, axis=1))
                        shift *= 2
                    return total

                top = over(parts, jnp.maximum)
                weights = [jnp.exp(v - top) for v in parts]
                inv = 1.0 / over(weights, jnp.add)
                score = over([w * v for w, v in zip(weights, parts)], jnp.add) * inv
                scores[at, :] = score
                rest = 1.0 - score
                scaled = inv * inv_scale
                for i, (w, v) in enumerate(zip(weights, parts)):
                    slopes[at, i * LANES:(i + 1) * LANES] = (w * scaled) * (v + rest)

    shared[0].wait_recv()
    forward([me, sibling])

    from_x[1].wait_recv()
    shared.append(pass_on(1, across))
    straight, other = [across], [device(y, 1 - x, 1 - par)]
    for k in mates:
        from_y[k][0].wait_recv()
        shared.append(pass_on(2 + k, device(downs[k], x, par)))
        straight.append(device(downs[k], x, par))
        other.append(device(downs[k], x, 1 - par))
    forward(straight)
    corner = []
    for k in mates:
        diag_y[k].wait_recv()
        diag_x[k].wait_recv()
        shared.append(pass_on(1 + tall + k, device(downs[k], 1 - x, par)))
        corner.append(device(downs[k], 1 - x, par))
    for copy in shared[1:1 + tall]:
        copy.wait_recv()
    forward(other)
    for k in mates:
        shared[1 + tall + k].wait_recv()
        corner.append(device(downs[k], 1 - x, 1 - par))
    forward(corner)

    all_scores = scores[...]
    top_score = jnp.max(all_scores, axis=0, keepdims=True)
    log_total = top_score + jnp.log(jnp.sum(jnp.exp(all_scores - top_score), axis=0, keepdims=True))
    get_gold.wait()
    gold = jnp.concatenate([gold_v[...]] * (LANES // ctx), axis=1)

    def block(b, picked):
        at = pl.ds(pl.multiple_of(b * batch, batch), batch)
        ids = lax.broadcasted_iota(jnp.int32, (batch, LANES), 0) + b * batch
        hot = jnp.where(ids == gold, 1.0, 0.0)
        score = scores[at, :]
        score_grad = jnp.exp(score - log_total) - hot
        for j in range(n_rows // LANES):
            lanes = slice(j * LANES, (j + 1) * LANES)
            grads[at, lanes] = (score_grad * slopes[at, lanes]).astype(BF16)
        return picked + jnp.sum(hot * score, axis=0, keepdims=True)

    picked = lax.fori_loop(0, ring, block, jnp.zeros((1, LANES), F32))
    loss_ref[...] = (log_total - picked)[:, :ctx]

    chunk = width // ring
    mid = cands // 2
    targets = ([(ups[k], 1 - x) for k in mates] + [(y, 1 - x)] + [(ups[k], x) for k in mates]
               + [(y, x)])
    at_x, at_y, at_me = tall - 1, tall, chips - 1
    sib, via_x, via_y = [], [], []
    in_x, in_y = [None, None], [[None, None] for _ in mates]

    def finish(s):
        sib[s].wait_recv()
        total = e_own[s, par].astype(F32) + e_sib[s].astype(F32)
        e_sum[s] = total.astype(BF16)
        low, high = e_sum.at[s, :mid], e_sum.at[s, mid:]
        if s < at_x:
            via_x.append(post(low, e_via_x.at[s], evx_send.at[s], evx_recv.at[s],
                              {"loop": across}))
            via_y.append(post(high, e_via_y.at[s], evy_send.at[s], evy_recv.at[s],
                              {"loop": device(ups[s], x, par)}))
        elif s == at_x:
            in_x[0] = post(low, e_x.at[0], ex_send.at[0], ex_recv.at[0], {"loop": across})
        elif s < at_me:
            k = s - at_y
            in_y[k][1] = post(high, e_y.at[k, 1], ey_send.at[k, 1], ey_recv.at[k, 1],
                              {"loop": device(ups[k], x, par)})

    for s, (yy, xx) in enumerate(targets):
        cols = pl.ds(pl.multiple_of((yy * 2 + xx) * 2 * chunk, 2 * chunk), 2 * chunk)
        part = dot(grads[...], rows[:, cols]).astype(BF16)
        e_own[s, 0] = part[:, :chunk]
        e_own[s, 1] = part[:, chunk:]
        sib.append(post(e_own.at[s, 1 - par], e_sib.at[s], es_send.at[s], es_recv.at[s],
                        {"loop": sibling}))
        if s >= LAG:
            finish(s - LAG)
    for s in range(chips - LAG, chips):
        finish(s)

    permutation(ctx, per)

    for k in mates:
        via_x[k].wait_recv()
        total = e_sum[at_y + k, :mid].astype(F32) + e_via_x[k].astype(F32)
        e_fwd_y[k] = total.astype(BF16)
        in_y[k][0] = post(e_fwd_y.at[k], e_y.at[k, 0], ey_send.at[k, 0], ey_recv.at[k, 0],
                          {"loop": device(ups[k], x, par)})
    total = e_sum[at_x, mid:].astype(F32)
    for k in mates:
        via_y[k].wait_recv()
        total = total + e_via_y[k].astype(F32)
    e_fwd_x[...] = total.astype(BF16)
    in_x[1] = post(e_fwd_x, e_x.at[1], ex_send.at[1], ex_recv.at[1], {"loop": across})

    for k in range(chips - 1):
        far[k].wait_recv()
        src = held.at[(chip + chips - 1 - k) % chips * 2 + par]
        near.append(post(src, src, hs_send.at[k], hs_recv.at[k], {"loop": sibling}))

    @pl.loop(0, cands // TILE)
    def _(t):
        cols = pl.ds(pl.multiple_of(t * TILE, TILE), TILE)
        gradt[:, cols] = lax.dot_general(
            perm[...], grads[cols, :], NT, preferred_element_type=F32).astype(BF16)

    for copy in near:
        copy.wait_recv()
    hid_all = held.reshape(cands, width)

    @pl.loop(0, width // LANES)
    def _(t):
        cols = pl.ds(pl.multiple_of(t * LANES, LANES), LANES)
        hidt[cols, :] = hid_all[:, cols].T

    halves = []
    for h in range(2):
        total = e_sum[at_me, h * mid:(h + 1) * mid].astype(F32)
        in_x[h].wait_recv()
        total = total + e_x[h].astype(F32)
        for k in mates:
            in_y[k][h].wait_recv()
            total = total + e_y[k, h].astype(F32)
        halves.append(total.astype(BF16))
    p_part = dot(hidt[...], jnp.concatenate(halves, axis=0))
    out_rows = q_in.shape[1]
    for g in range(groups):
        for l in range(ring):
            first = (l * groups + g) * out_rows
            p_own[g, l] = p_part[first:first + out_rows].astype(BF16)
    z_far = []
    for k in range(groups - 1):
        to = (group + 1 + k) % groups
        z_far.append(post(p_own.at[to], p_in.at[k], z_send.at[k], z_recv.at[k], {"dp": to}))

    @pl.loop(0, n_rows // TILE)
    def _(t):
        at = pl.ds(pl.multiple_of(t * TILE, TILE), TILE)
        code_ref[at, :] = dot(gradt[at, :], embed[...])

    total = p_own[group].astype(F32)
    for k in range(groups - 1):
        z_far[k].wait_recv()
        total = total + p_in[k].astype(F32)
    q_own[...] = total.astype(BF16)
    q_far = []
    for k in range(ring - 1):
        to = (me + 1 + k) % ring
        q_far.append(post(q_own.at[to], q_in.at[me], q_send.at[k], q_recv.at[k], {"loop": to}))
    q_in[me] = q_own[me]
    for k in range(ring - 1):
        q_far[k].wait_recv()
    for l in range(ring):
        proj_out[:, l * chunk:(l + 1) * chunk] = q_in[l].astype(F32)
    for copy in started:
        copy.wait_send()


def write_body(code_ref, loss_ref, proj_ref, code_out, loss_out, proj_out, sems):
    parts = sems.shape[0] - 2
    step = code_ref.shape[0] // parts
    copies = [
        pltpu.make_async_copy(code_ref.at[pl.ds(i * step, step)], code_out.at[pl.ds(i * step, step)],
                              sems.at[i])
        for i in range(parts)
    ]
    copies.append(pltpu.make_async_copy(proj_ref, proj_out, sems.at[parts]))
    copies.append(pltpu.make_async_copy(loss_ref, loss_out, sems.at[parts + 1]))
    for copy in copies:
        copy.start()
    for copy in copies:
        copy.wait()


def local(ring, groups, codes, cand_hidden, proj, gold):
    ctx, per, width = codes.shape
    batch = cand_hidden.shape[0]
    n_rows = ctx * per
    chips = ring // 2
    mates = chips // 2 - 1
    cands = ring * batch
    out_rows = width // (ring * groups)
    chunk = width // ring
    vmem = pl.BlockSpec(memory_space=pltpu.VMEM)
    hbm = pl.BlockSpec(memory_space=pltpu.HBM)
    dma = pltpu.SemaphoreType.DMA
    results = (
        jax.ShapeDtypeStruct((1, ctx), F32),
        jax.ShapeDtypeStruct((n_rows, width), F32),
        jax.ShapeDtypeStruct((out_rows, width), F32),
    )
    inputs = [pltpu.with_memory_space_constraint(v, pltpu.HBM) for v in (
        codes.reshape(n_rows, width), cand_hidden, proj, gold.reshape(1, ctx))]
    loss, code_grad, proj_grad = pl.pallas_call(
        functools.partial(body, ring, groups, ctx, per),
        name="link_step",
        out_shape=results,
        in_specs=[hbm, hbm, hbm, hbm],
        out_specs=(vmem, vmem, vmem),
        scratch_shapes=[
            pltpu.VMEM((n_rows, width), BF16),
            pltpu.VMEM((width, width), BF16),
            pltpu.VMEM((1, ctx), jnp.int32),
            pltpu.VMEM((n_rows, n_rows), BF16),
            pltpu.VMEM((n_rows, width), BF16),
            pltpu.VMEM((ring, batch, width), BF16),
            pltpu.VMEM((cands, width), BF16),
            pltpu.VMEM((2 * (chips // 2) * batch, n_rows), F32),
            pltpu.VMEM((cands, n_rows), F32),
            pltpu.VMEM((cands, LANES), F32),
            pltpu.VMEM((cands, n_rows), BF16),
            pltpu.VMEM((n_rows, cands), BF16),
            pltpu.VMEM((width, cands), BF16),
            pltpu.VMEM((chips, 2, cands, chunk), BF16),
            pltpu.VMEM((chips, cands, chunk), BF16),
            pltpu.VMEM((chips, cands, chunk), BF16),
            pltpu.VMEM((mates, cands // 2, chunk), BF16),
            pltpu.VMEM((mates, cands // 2, chunk), BF16),
            pltpu.VMEM((2, cands // 2, chunk), BF16),
            pltpu.VMEM((mates, 2, cands // 2, chunk), BF16),
            pltpu.VMEM((cands // 2, chunk), BF16),
            pltpu.VMEM((mates, cands // 2, chunk), BF16),
            pltpu.VMEM((groups, ring, out_rows, chunk), BF16),
            pltpu.VMEM((groups - 1, ring, out_rows, chunk), BF16),
            pltpu.VMEM((ring, out_rows, chunk), BF16),
            pltpu.VMEM((ring, out_rows, chunk), BF16),
            dma((3,)), dma((width // TILE,)),
            dma((2,)), dma((2,)), dma((mates, 2)), dma((mates, 2)),
            dma((mates,)), dma((mates,)), dma((mates,)), dma((mates,)),
            dma((chips,)), dma((chips,)),
            dma((chips - 1,)), dma((chips - 1,)), dma((chips,)), dma((chips,)),
            dma((chips,)), dma((chips,)),
            dma((mates,)), dma((mates,)), dma((mates,)), dma((mates,)),
            dma((2,)), dma((2,)), dma((mates, 2)), dma((mates, 2)),
            dma((groups - 1,)), dma((groups - 1,)),
            dma((ring - 1,)), dma((ring - 1,)),
        ],
        compiler_params=pltpu.CompilerParams(
            collective_id=0, has_side_effects=True, vmem_limit_bytes=44 * 2**20),
    )(*inputs)
    code_grad, loss, proj_grad = pl.pallas_call(
        write_body,
        name="code_grad",
        out_shape=(results[1], results[0], results[2]),
        in_specs=[vmem, vmem, vmem],
        out_specs=(pl.BlockSpec(memory_space=pl.ANY),) * 3,
        scratch_shapes=[dma((8 + 2,))],
        compiler_params=pltpu.CompilerParams(vmem_limit_bytes=8 * 2**20),
    )(code_grad, loss, proj_grad)
    return loss.reshape(ctx), code_grad.reshape(ctx, per, width), proj_grad


def solution(mesh):
    return jax.shard_map(
        functools.partial(local, mesh.shape["loop"], mesh.shape["dp"]),
        mesh=mesh,
        in_specs=(P(("loop", "dp"), None, None), P(("loop", "dp"), None), P(), P(("loop", "dp"))),
        out_specs=(P(("loop", "dp")), P(("loop", "dp"), None, None), P(("loop", "dp"), None)),
        check_vma=False,
    )
```

```python
import functools

import jax
import jax.numpy as jnp
from jax import lax
from jax.experimental import pallas as pl
from jax.experimental.pallas import tpu as pltpu
from jax.sharding import PartitionSpec as P

MESH = pl.DeviceIdType.MESH
F32 = jnp.float32
BF16 = jnp.bfloat16
LANES = 128
STEP = 16
TILE = 256
LAG = 2
NT = (((1,), (1,)), ((), ()))


def dot(a, b):
    return jnp.dot(a, b, preferred_element_type=F32)


def body(
    ring, groups, ctx, per,
    codes_ref, hidden_ref, proj_ref, gold_ref,
    loss_ref, code_ref, proj_out,
    codes, proj, gold_v, perm, rows, held, embed, logits, slopes, scores, grads, gradt, hidt,
    e_own, e_sib, e_sum, e_via_x, e_via_y, e_x, e_y, e_fwd_x, e_fwd_y,
    p_own, p_in,
    local_sem, proj_sem,
    bx_send, bx_recv, by_send, by_recv, bdx_send, bdx_recv, bdy_send, bdy_recv,
    bs_send, bs_recv, h_send, h_recv, hs_send, hs_recv, es_send, es_recv,
    evx_send, evx_recv, evy_send, evy_recv, ex_send, ex_recv, ey_send, ey_recv,
    p_send, p_recv, ready,
):
    batch, width = hidden_ref.shape
    chips = ring // 2
    tall = chips // 2
    cands = ring * batch
    n_rows = ctx * per
    me = lax.axis_index("loop")
    group = lax.axis_index("dp")
    chip, par = me // 2, me % 2
    y, x = chip // 2, chip % 2
    inv_scale = width ** -0.5

    def device(yy, xx, pp):
        return (yy * 2 + xx) * 2 + pp

    sibling = device(y, x, 1 - par)
    across = device(y, 1 - x, par)
    mates = range(tall - 1)
    ups = [(y + 1 + k) % tall for k in mates]
    downs = [(y + tall - 1 - k) % tall for k in mates]

    barrier = pltpu.get_barrier_semaphore()
    for k in range(1, ring):
        pl.semaphore_signal(barrier, 1, device_id={"loop": (me + k) % ring}, device_id_type=MESH)
    for k in range(1, groups):
        pl.semaphore_signal(barrier, 1, device_id={"dp": (group + k) % groups}, device_id_type=MESH)

    get_hidden = pltpu.make_async_copy(hidden_ref, held.at[me], local_sem.at[0])
    get_hidden.start()
    get_proj = []
    for t in range(width // TILE):
        cols = slice(t * TILE, (t + 1) * TILE)
        copy = pltpu.make_async_copy(proj_ref.at[:, cols], proj.at[:, cols], proj_sem.at[t])
        copy.start()
        get_proj.append(copy)
    get_codes = pltpu.make_async_copy(codes_ref, codes, local_sem.at[1])
    get_gold = pltpu.make_async_copy(gold_ref, gold_v, local_sem.at[2])
    get_gold.start()

    row_tile = 128

    def permutation(outer, inner):
        @pl.loop(0, n_rows // row_tile)
        def _(t):
            start = pl.multiple_of(t * row_tile, row_tile)
            r = lax.broadcasted_iota(jnp.int32, (row_tile, n_rows), 0) + start
            c = lax.broadcasted_iota(jnp.int32, (row_tile, n_rows), 1)
            perm[pl.ds(start, row_tile), :] = jnp.where(
                c == (r % inner) * outer + r // inner, 1.0, 0.0).astype(BF16)

    permutation(per, ctx)

    def send(src, dst, ssem, rsem, where):
        copy = pltpu.make_async_remote_copy(
            src_ref=src, dst_ref=dst, send_sem=ssem, recv_sem=rsem,
            device_id=where, device_id_type=MESH)
        copy.start()
        return copy

    def spot_of(owner):
        return pl.ds(pl.multiple_of(owner * batch, batch), batch)

    piece = batch // 2

    def piece_of(owner, part):
        return embed.at[pl.ds(pl.multiple_of(owner * batch + part * piece, piece), piece)]

    get_hidden.wait()
    for t in range(width // TILE):
        cols = slice(t * TILE, (t + 1) * TILE)
        get_proj[t].wait()
        if t == 0:
            get_codes.start()
        embed[spot_of(me), cols] = dot(held[me], proj[:, cols]).astype(BF16)
    pl.semaphore_wait(barrier, ring + groups - 2)
    for k in range(1, ring):
        pl.semaphore_signal(ready, 1, device_id={"loop": (me + k) % ring}, device_id_type=MESH)

    started = []

    def post(*args):
        copy = send(*args)
        started.append(copy)
        return copy

    def pass_on(slot, owner):
        block = embed.at[spot_of(owner)]
        return post(block, block, bs_send.at[slot], bs_recv.at[slot], {"loop": sibling})

    own = [piece_of(me, 0), piece_of(me, 1)]
    from_x, from_y = [None, None], [[None, None] for _ in mates]

    def show(first):
        last = 1 - first
        from_x[first] = post(own[first], own[first], bx_send.at[first], bx_recv.at[first],
                             {"loop": across})
        for k in mates:
            from_y[k][last] = post(own[last], own[last], by_send.at[k, last],
                                   by_recv.at[k, last], {"loop": device(ups[k], x, par)})

    def reorder(first, last):
        @pl.loop(first, last)
        def _(t):
            cols = pl.ds(pl.multiple_of(t * TILE, TILE), TILE)
            rows[:, cols] = dot(perm[...], codes[:, cols]).astype(BF16)

    show(0)
    shared = [pass_on(0, me)]
    get_codes.wait()
    tiles = width // TILE
    reorder(0, tiles // 2)
    show(1)
    reorder(tiles // 2, tiles)

    diag_y, diag_x = [], []
    from_x[0].wait_recv()
    for k in mates:
        block = piece_of(across, 0)
        diag_y.append(post(block, block, bdy_send.at[k], bdy_recv.at[k],
                           {"loop": device(ups[k], x, par)}))
    for k in mates:
        from_y[k][1].wait_recv()
        block = piece_of(device(downs[k], x, par), 1)
        diag_x.append(post(block, block, bdx_send.at[k], bdx_recv.at[k], {"loop": across}))

    def over(values, op):
        while len(values) > 1:
            values = [op(*values[i:i + 2]) if i + 1 < len(values) else values[i]
                      for i in range(0, len(values), 2)]
        total = values[0]
        shift = ctx
        while shift < LANES:
            total = op(total, pltpu.roll(total, shift, axis=1))
            shift *= 2
        return total

    def soften(held_logits, src, at):
        parts = [held_logits[src:src + STEP, i * LANES:(i + 1) * LANES]
                 for i in range(n_rows // LANES)]
        top = over(parts, jnp.maximum)
        weights = [jnp.exp(v - top) for v in parts]
        inv = 1.0 / over(weights, jnp.add)
        score = over([w * v for w, v in zip(weights, parts)], jnp.add) * inv
        at = pl.ds(pl.multiple_of(at, STEP), STEP)
        scores[at, :] = score
        rest = 1.0 - score
        scaled = inv * inv_scale
        for i, (w, v) in enumerate(zip(weights, parts)):
            slopes[at, i * LANES:(i + 1) * LANES] = (w * scaled) * (v + rest)

    waiting = []

    def forward(owners):
        stage = forward.stage
        forward.stage += 1
        count = len(owners) * batch
        spots = [spot_of(o) for o in owners]
        previous, waiting[:] = list(waiting), [
            (stage % 2, j * batch + r, o * batch + r)
            for j, o in enumerate(owners) for r in range(0, batch, STEP)]
        turns = n_rows // TILE
        for t in range(turns):
            if owners:
                cols = slice(t * TILE, (t + 1) * TILE)
                logits[stage % 2, :count, cols] = lax.dot_general(
                    jnp.concatenate([embed[spot, :] for spot in spots], axis=0), rows[cols, :], NT,
                    preferred_element_type=F32) * inv_scale
            some = -(-len(previous) // turns)
            for slot, src, at in previous[t * some:(t + 1) * some]:
                soften(logits.at[slot], src, at)

    forward.stage = 0

    shared[0].wait_recv()
    forward([me, sibling])

    from_x[1].wait_recv()
    shared.append(pass_on(1, across))
    straight, other = [across], [device(y, 1 - x, 1 - par)]
    for k in mates:
        from_y[k][0].wait_recv()
        shared.append(pass_on(2 + k, device(downs[k], x, par)))
        straight.append(device(downs[k], x, par))
        other.append(device(downs[k], x, 1 - par))
    forward(straight)
    corner = []
    for k in mates:
        diag_y[k].wait_recv()
        diag_x[k].wait_recv()
        shared.append(pass_on(1 + tall + k, device(downs[k], 1 - x, par)))
        corner.append(device(downs[k], 1 - x, par))
    far = []
    for k in range(chips - 1):
        to = (chip + 1 + k) % chips
        far.append(post(hidden_ref, held.at[me], h_send.at[k], h_recv.at[k],
                        {"loop": to * 2 + par}))
    near = [post(hidden_ref, held.at[me], hs_send.at[chips - 1], hs_recv.at[chips - 1],
                 {"loop": sibling})]
    for copy in shared[1:1 + tall]:
        copy.wait_recv()
    forward(other)
    for k in mates:
        shared[1 + tall + k].wait_recv()
        corner.append(device(downs[k], 1 - x, 1 - par))
    forward(corner)
    forward([])

    all_scores = scores[...]
    top_score = jnp.max(all_scores, axis=0, keepdims=True)
    log_total = top_score + jnp.log(jnp.sum(jnp.exp(all_scores - top_score), axis=0, keepdims=True))
    get_gold.wait()
    gold = jnp.concatenate([gold_v[...]] * (LANES // ctx), axis=1)

    def block(b, picked):
        at = pl.ds(pl.multiple_of(b * batch, batch), batch)
        ids = lax.broadcasted_iota(jnp.int32, (batch, LANES), 0) + b * batch
        hot = jnp.where(ids == gold, 1.0, 0.0)
        score = scores[at, :]
        score_grad = jnp.exp(score - log_total) - hot
        for j in range(n_rows // LANES):
            lanes = slice(j * LANES, (j + 1) * LANES)
            grads[at, lanes] = (score_grad * slopes[at, lanes]).astype(BF16)
        return picked + jnp.sum(hot * score, axis=0, keepdims=True)

    picked = lax.fori_loop(0, ring, block, jnp.zeros((1, LANES), F32))
    loss_ref[...] = (log_total - picked)[:, :ctx]

    chunk = width // ring
    mid = cands // 2
    targets = ([(ups[k], 1 - x) for k in mates] + [(y, 1 - x)] + [(ups[k], x) for k in mates]
               + [(y, x)])
    at_x, at_y, at_me = tall - 1, tall, chips - 1
    sib, via_x, via_y = [], [], []
    in_x, in_y = [None, None], [[None, None] for _ in mates]

    def finish(s):
        sib[s].wait_recv()
        total = e_own[s, par].astype(F32) + e_sib[s].astype(F32)
        e_sum[s] = total.astype(BF16)
        low, high = e_sum.at[s, :mid], e_sum.at[s, mid:]
        if s < at_x:
            via_x.append(post(low, e_via_x.at[s], evx_send.at[s], evx_recv.at[s],
                              {"loop": across}))
            via_y.append(post(high, e_via_y.at[s], evy_send.at[s], evy_recv.at[s],
                              {"loop": device(ups[s], x, par)}))
        elif s == at_x:
            in_x[0] = post(low, e_x.at[0], ex_send.at[0], ex_recv.at[0], {"loop": across})
        elif s < at_me:
            k = s - at_y
            in_y[k][1] = post(high, e_y.at[k, 1], ey_send.at[k, 1], ey_recv.at[k, 1],
                              {"loop": device(ups[k], x, par)})

    for s, (yy, xx) in enumerate(targets):
        cols = pl.ds(pl.multiple_of((yy * 2 + xx) * 2 * chunk, 2 * chunk), 2 * chunk)
        part = dot(grads[...], rows[:, cols]).astype(BF16)
        e_own[s, 0] = part[:, :chunk]
        e_own[s, 1] = part[:, chunk:]
        sib.append(post(e_own.at[s, 1 - par], e_sib.at[s], es_send.at[s], es_recv.at[s],
                        {"loop": sibling}))
        if s >= LAG:
            finish(s - LAG)
    for s in range(chips - LAG, chips):
        finish(s)

    permutation(ctx, per)

    for k in mates:
        via_x[k].wait_recv()
        total = e_sum[at_y + k, :mid].astype(F32) + e_via_x[k].astype(F32)
        e_fwd_y[k] = total.astype(BF16)
        in_y[k][0] = post(e_fwd_y.at[k], e_y.at[k, 0], ey_send.at[k, 0], ey_recv.at[k, 0],
                          {"loop": device(ups[k], x, par)})
    total = e_sum[at_x, mid:].astype(F32)
    for k in mates:
        via_y[k].wait_recv()
        total = total + e_via_y[k].astype(F32)
    e_fwd_x[...] = total.astype(BF16)
    in_x[1] = post(e_fwd_x, e_x.at[1], ex_send.at[1], ex_recv.at[1], {"loop": across})

    for k in range(chips - 1):
        far[k].wait_recv()
        src = held.at[(chip + chips - 1 - k) % chips * 2 + par]
        near.append(post(src, src, hs_send.at[k], hs_recv.at[k], {"loop": sibling}))

    @pl.loop(0, cands // TILE)
    def _(t):
        cols = pl.ds(pl.multiple_of(t * TILE, TILE), TILE)
        gradt[:, cols] = lax.dot_general(
            perm[...], grads[cols, :], NT, preferred_element_type=F32).astype(BF16)

    for copy in near:
        copy.wait_recv()
    hid_all = held.reshape(cands, width)

    @pl.loop(0, width // LANES)
    def _(t):
        cols = pl.ds(pl.multiple_of(t * LANES, LANES), LANES)
        hidt[cols, :] = hid_all[:, cols].T

    halves = []
    for h in range(2):
        total = e_sum[at_me, h * mid:(h + 1) * mid].astype(F32)
        in_x[h].wait_recv()
        total = total + e_x[h].astype(F32)
        for k in mates:
            in_y[k][h].wait_recv()
            total = total + e_y[k, h].astype(F32)
        halves.append(total.astype(BF16))
    p_part = dot(hidt[...], jnp.concatenate(halves, axis=0))
    out_rows = proj_out.shape[0]
    for g in range(groups):
        for l in range(ring):
            first = (l * groups + g) * out_rows
            p_own[g, l] = p_part[first:first + out_rows].astype(BF16)
    pl.semaphore_wait(ready, ring - 1)

    def outgoing(k):
        to, there = (me + k % ring) % ring, (group + k // ring) % groups
        return pltpu.make_async_remote_copy(
            src_ref=p_own.at[there, to], dst_ref=p_in.at[k], send_sem=p_send.at[k],
            recv_sem=p_recv.at[k], device_id={"loop": to, "dp": there}, device_id_type=MESH)

    @pl.loop(ring, ring * groups)
    def _(k):
        outgoing(k).start()

    @pl.loop(1, ring)
    def _(k):
        outgoing(k).start()

    @pl.loop(0, n_rows // TILE)
    def _(t):
        at = pl.ds(pl.multiple_of(t * TILE, TILE), TILE)
        code_ref[at, :] = dot(gradt[at, :], embed[...])

    p_in[0] = p_own[group, me]

    @pl.loop(1, ring * groups)
    def _(k):
        outgoing(k).wait_recv()

    for l in range(ring):
        slot = (me + ring - l) % ring
        total = p_in[slot].astype(F32)
        for g in range(1, groups):
            total = total + p_in[g * ring + slot].astype(F32)
        proj_out[:, l * chunk:(l + 1) * chunk] = total

    @pl.loop(1, ring * groups)
    def _(k):
        outgoing(k).wait_send()

    for copy in started:
        copy.wait_send()


def write_body(code_ref, loss_ref, proj_ref, code_out, loss_out, proj_out, sems):
    parts = sems.shape[0] - 2
    step = code_ref.shape[0] // parts
    copies = [
        pltpu.make_async_copy(code_ref.at[pl.ds(i * step, step)], code_out.at[pl.ds(i * step, step)],
                              sems.at[i])
        for i in range(parts)
    ]
    copies.append(pltpu.make_async_copy(proj_ref, proj_out, sems.at[parts]))
    copies.append(pltpu.make_async_copy(loss_ref, loss_out, sems.at[parts + 1]))
    for copy in copies:
        copy.start()
    for copy in copies:
        copy.wait()


def local(ring, groups, codes, cand_hidden, proj, gold):
    ctx, per, width = codes.shape
    batch = cand_hidden.shape[0]
    n_rows = ctx * per
    chips = ring // 2
    mates = chips // 2 - 1
    cands = ring * batch
    out_rows = width // (ring * groups)
    chunk = width // ring
    vmem = pl.BlockSpec(memory_space=pltpu.VMEM)
    hbm = pl.BlockSpec(memory_space=pltpu.HBM)
    dma = pltpu.SemaphoreType.DMA
    results = (
        jax.ShapeDtypeStruct((1, ctx), F32),
        jax.ShapeDtypeStruct((n_rows, width), F32),
        jax.ShapeDtypeStruct((out_rows, width), F32),
    )
    inputs = [pltpu.with_memory_space_constraint(v, pltpu.HBM) for v in (
        codes.reshape(n_rows, width), cand_hidden, proj, gold.reshape(1, ctx))]
    loss, code_grad, proj_grad = pl.pallas_call(
        functools.partial(body, ring, groups, ctx, per),
        name="link_step",
        out_shape=results,
        in_specs=[hbm, hbm, hbm, hbm],
        out_specs=(vmem, vmem, vmem),
        scratch_shapes=[
            pltpu.VMEM((n_rows, width), BF16),
            pltpu.VMEM((width, width), BF16),
            pltpu.VMEM((1, ctx), jnp.int32),
            pltpu.VMEM((n_rows, n_rows), BF16),
            pltpu.VMEM((n_rows, width), BF16),
            pltpu.VMEM((ring, batch, width), BF16),
            pltpu.VMEM((cands, width), BF16),
            pltpu.VMEM((2, chips * batch, n_rows), F32),
            pltpu.VMEM((cands, n_rows), F32),
            pltpu.VMEM((cands, LANES), F32),
            pltpu.VMEM((cands, n_rows), BF16),
            pltpu.VMEM((n_rows, cands), BF16),
            pltpu.VMEM((width, cands), BF16),
            pltpu.VMEM((chips, 2, cands, chunk), BF16),
            pltpu.VMEM((chips, cands, chunk), BF16),
            pltpu.VMEM((chips, cands, chunk), BF16),
            pltpu.VMEM((mates, cands // 2, chunk), BF16),
            pltpu.VMEM((mates, cands // 2, chunk), BF16),
            pltpu.VMEM((2, cands // 2, chunk), BF16),
            pltpu.VMEM((mates, 2, cands // 2, chunk), BF16),
            pltpu.VMEM((cands // 2, chunk), BF16),
            pltpu.VMEM((mates, cands // 2, chunk), BF16),
            pltpu.VMEM((groups, ring, out_rows, chunk), BF16),
            pltpu.VMEM((groups * ring, out_rows, chunk), BF16),
            dma((3,)), dma((width // TILE,)),
            dma((2,)), dma((2,)), dma((mates, 2)), dma((mates, 2)),
            dma((mates,)), dma((mates,)), dma((mates,)), dma((mates,)),
            dma((chips,)), dma((chips,)),
            dma((chips - 1,)), dma((chips - 1,)), dma((chips,)), dma((chips,)),
            dma((chips,)), dma((chips,)),
            dma((mates,)), dma((mates,)), dma((mates,)), dma((mates,)),
            dma((2,)), dma((2,)), dma((mates, 2)), dma((mates, 2)),
            dma((groups * ring,)), dma((groups * ring,)), pltpu.SemaphoreType.REGULAR,
        ],
        compiler_params=pltpu.CompilerParams(
            collective_id=0, has_side_effects=True, vmem_limit_bytes=44 * 2**20),
    )(*inputs)
    code_grad, loss, proj_grad = pl.pallas_call(
        write_body,
        name="code_grad",
        out_shape=(results[1], results[0], results[2]),
        in_specs=[vmem, vmem, vmem],
        out_specs=(pl.BlockSpec(memory_space=pl.ANY),) * 3,
        scratch_shapes=[dma((8 + 2,))],
        compiler_params=pltpu.CompilerParams(vmem_limit_bytes=8 * 2**20),
    )(code_grad, loss, proj_grad)
    return loss.reshape(ctx), code_grad.reshape(ctx, per, width), proj_grad


def solution(mesh):
    return jax.shard_map(
        functools.partial(local, mesh.shape["loop"], mesh.shape["dp"]),
        mesh=mesh,
        in_specs=(P(("loop", "dp"), None, None), P(("loop", "dp"), None), P(), P(("loop", "dp"))),
        out_specs=(P(("loop", "dp")), P(("loop", "dp"), None, None), P(("loop", "dp"), None)),
        check_vma=False,
    )
```

```python
import functools

import jax
import jax.numpy as jnp
from jax import lax
from jax.experimental import pallas as pl
from jax.experimental.pallas import tpu as pltpu
from jax.sharding import PartitionSpec as P

MESH = pl.DeviceIdType.MESH
F32 = jnp.float32
BF16 = jnp.bfloat16
LANES = 128
STEP = 16
TILE = 256
NT = (((1,), (1,)), ((), ()))


def dot(a, b):
    return jnp.dot(a, b, preferred_element_type=F32)


def body(
    ring, groups, ctx, per,
    codes_ref, hidden_ref, proj_ref, gold_ref,
    loss_ref, code_ref, proj_out,
    codes, proj, gold_v, perm, rows, held, embed, logits, slopes, scores, grads, gradt, hidt,
    e_own, e_sib, e_sum, e_via_x, e_via_y, e_x, e_y, e_fwd_x, e_fwd_y,
    p_own, p_in,
    local_sem, proj_sem,
    bx_send, bx_recv, by_send, by_recv, bdx_send, bdx_recv, bdy_send, bdy_recv,
    bs_send, bs_recv, h_send, h_recv, hs_send, hs_recv, es_send, es_recv,
    evx_send, evx_recv, evy_send, evy_recv, ex_send, ex_recv, ey_send, ey_recv,
    p_send, p_recv, ready,
):
    batch, width = hidden_ref.shape
    chips = ring // 2
    tall = chips // 2
    cands = ring * batch
    n_rows = ctx * per
    me = lax.axis_index("loop")
    group = lax.axis_index("dp")
    chip, par = me // 2, me % 2
    y, x = chip // 2, chip % 2
    inv_scale = width ** -0.5

    def device(yy, xx, pp):
        return (yy * 2 + xx) * 2 + pp

    sibling = device(y, x, 1 - par)
    across = device(y, 1 - x, par)
    mates = range(tall - 1)
    ups = [(y + 1 + k) % tall for k in mates]
    downs = [(y + tall - 1 - k) % tall for k in mates]

    barrier = pltpu.get_barrier_semaphore()
    for k in range(1, ring):
        pl.semaphore_signal(barrier, 1, device_id={"loop": (me + k) % ring}, device_id_type=MESH)
    for k in range(1, groups):
        pl.semaphore_signal(barrier, 1, device_id={"dp": (group + k) % groups}, device_id_type=MESH)

    get_hidden = pltpu.make_async_copy(hidden_ref, held.at[me], local_sem.at[0])
    get_hidden.start()
    get_proj = []
    for t in range(width // TILE):
        cols = slice(t * TILE, (t + 1) * TILE)
        copy = pltpu.make_async_copy(proj_ref.at[:, cols], proj.at[:, cols], proj_sem.at[t])
        copy.start()
        get_proj.append(copy)
    get_codes = pltpu.make_async_copy(codes_ref, codes, local_sem.at[1])
    get_gold = pltpu.make_async_copy(gold_ref, gold_v, local_sem.at[2])
    get_gold.start()

    row_tile = 128

    def permutation(outer, inner):
        @pl.loop(0, n_rows // row_tile)
        def _(t):
            start = pl.multiple_of(t * row_tile, row_tile)
            r = lax.broadcasted_iota(jnp.int32, (row_tile, n_rows), 0) + start
            c = lax.broadcasted_iota(jnp.int32, (row_tile, n_rows), 1)
            perm[pl.ds(start, row_tile), :] = jnp.where(
                c == (r % inner) * outer + r // inner, 1.0, 0.0).astype(BF16)

    permutation(per, ctx)

    def send(src, dst, ssem, rsem, where):
        copy = pltpu.make_async_remote_copy(
            src_ref=src, dst_ref=dst, send_sem=ssem, recv_sem=rsem,
            device_id=where, device_id_type=MESH)
        copy.start()
        return copy

    def spot_of(owner):
        return pl.ds(pl.multiple_of(owner * batch, batch), batch)

    piece = batch // 2

    def piece_of(owner, part):
        return embed.at[pl.ds(pl.multiple_of(owner * batch + part * piece, piece), piece)]

    get_hidden.wait()
    for t in range(width // TILE):
        cols = slice(t * TILE, (t + 1) * TILE)
        get_proj[t].wait()
        if t == 0:
            get_codes.start()
        embed[spot_of(me), cols] = dot(held[me], proj[:, cols]).astype(BF16)
    pl.semaphore_wait(barrier, ring + groups - 2)
    for k in range(1, ring):
        pl.semaphore_signal(ready, 1, device_id={"loop": (me + k) % ring}, device_id_type=MESH)

    started = []

    def post(*args):
        copy = send(*args)
        started.append(copy)
        return copy

    def pass_on(slot, owner):
        block = embed.at[spot_of(owner)]
        return post(block, block, bs_send.at[slot], bs_recv.at[slot], {"loop": sibling})

    own = [piece_of(me, 0), piece_of(me, 1)]
    from_x, from_y = [None, None], [[None, None] for _ in mates]

    def show(first):
        last = 1 - first
        from_x[first] = post(own[first], own[first], bx_send.at[first], bx_recv.at[first],
                             {"loop": across})
        for k in mates:
            from_y[k][last] = post(own[last], own[last], by_send.at[k, last],
                                   by_recv.at[k, last], {"loop": device(ups[k], x, par)})

    def reorder(first, last):
        @pl.loop(first, last)
        def _(t):
            cols = pl.ds(pl.multiple_of(t * TILE, TILE), TILE)
            rows[:, cols] = dot(perm[...], codes[:, cols]).astype(BF16)

    show(0)
    shared = [pass_on(0, me)]
    get_codes.wait()
    tiles = width // TILE
    reorder(0, tiles // 2)
    show(1)
    reorder(tiles // 2, tiles)

    diag_y, diag_x = [], []
    from_x[0].wait_recv()
    for k in mates:
        block = piece_of(across, 0)
        diag_y.append(post(block, block, bdy_send.at[k], bdy_recv.at[k],
                           {"loop": device(ups[k], x, par)}))
    for k in mates:
        from_y[k][1].wait_recv()
        block = piece_of(device(downs[k], x, par), 1)
        diag_x.append(post(block, block, bdx_send.at[k], bdx_recv.at[k], {"loop": across}))

    def over(values, op):
        while len(values) > 1:
            values = [op(*values[i:i + 2]) if i + 1 < len(values) else values[i]
                      for i in range(0, len(values), 2)]
        total = values[0]
        shift = ctx
        while shift < LANES:
            total = op(total, pltpu.roll(total, shift, axis=1))
            shift *= 2
        return total

    def soften(held_logits, src, at):
        parts = [held_logits[src:src + STEP, i * LANES:(i + 1) * LANES]
                 for i in range(n_rows // LANES)]
        top = over(parts, jnp.maximum)
        weights = [jnp.exp(v - top) for v in parts]
        inv = 1.0 / over(weights, jnp.add)
        score = over([w * v for w, v in zip(weights, parts)], jnp.add) * inv
        at = pl.ds(pl.multiple_of(at, STEP), STEP)
        scores[at, :] = score
        rest = 1.0 - score
        scaled = inv * inv_scale
        for i, (w, v) in enumerate(zip(weights, parts)):
            slopes[at, i * LANES:(i + 1) * LANES] = (w * scaled) * (v + rest)

    waiting = []

    def forward(owners):
        stage = forward.stage
        forward.stage += 1
        count = len(owners) * batch
        spots = [spot_of(o) for o in owners]
        previous, waiting[:] = list(waiting), [
            (stage % 2, j * batch + r, o * batch + r)
            for j, o in enumerate(owners) for r in range(0, batch, STEP)]
        turns = n_rows // TILE
        for t in range(turns):
            if owners:
                cols = slice(t * TILE, (t + 1) * TILE)
                logits[stage % 2, :count, cols] = lax.dot_general(
                    jnp.concatenate([embed[spot, :] for spot in spots], axis=0), rows[cols, :], NT,
                    preferred_element_type=F32) * inv_scale
            some = -(-len(previous) // turns)
            for slot, src, at in previous[t * some:(t + 1) * some]:
                soften(logits.at[slot], src, at)

    forward.stage = 0

    shared[0].wait_recv()
    forward([me, sibling])

    from_x[1].wait_recv()
    shared.append(pass_on(1, across))
    straight, other = [across], [device(y, 1 - x, 1 - par)]
    for k in mates:
        from_y[k][0].wait_recv()
        shared.append(pass_on(2 + k, device(downs[k], x, par)))
        straight.append(device(downs[k], x, par))
        other.append(device(downs[k], x, 1 - par))
    forward(straight)
    corner = []
    for k in mates:
        diag_y[k].wait_recv()
        diag_x[k].wait_recv()
        shared.append(pass_on(1 + tall + k, device(downs[k], 1 - x, par)))
        corner.append(device(downs[k], 1 - x, par))
    far = []
    for k in range(chips - 1):
        to = (chip + 1 + k) % chips
        far.append(post(hidden_ref, held.at[me], h_send.at[k], h_recv.at[k],
                        {"loop": to * 2 + par}))
    near = [post(hidden_ref, held.at[me], hs_send.at[chips - 1], hs_recv.at[chips - 1],
                 {"loop": sibling})]
    for copy in shared[1:1 + tall]:
        copy.wait_recv()
    forward(other)
    for k in mates:
        shared[1 + tall + k].wait_recv()
        corner.append(device(downs[k], 1 - x, 1 - par))
    forward(corner)
    forward([])

    all_scores = scores[...]
    top_score = jnp.max(all_scores, axis=0, keepdims=True)
    log_total = top_score + jnp.log(jnp.sum(jnp.exp(all_scores - top_score), axis=0, keepdims=True))
    get_gold.wait()
    gold = jnp.concatenate([gold_v[...]] * (LANES // ctx), axis=1)

    def block(b, picked):
        at = pl.ds(pl.multiple_of(b * batch, batch), batch)
        ids = lax.broadcasted_iota(jnp.int32, (batch, LANES), 0) + b * batch
        hot = jnp.where(ids == gold, 1.0, 0.0)
        score = scores[at, :]
        score_grad = jnp.exp(score - log_total) - hot
        for j in range(n_rows // LANES):
            lanes = slice(j * LANES, (j + 1) * LANES)
            grads[at, lanes] = (score_grad * slopes[at, lanes]).astype(BF16)
        return picked + jnp.sum(hot * score, axis=0, keepdims=True)

    picked = lax.fori_loop(0, ring, block, jnp.zeros((1, LANES), F32))
    loss_ref[...] = (log_total - picked)[:, :ctx]

    chunk = width // ring
    mid = cands // 2
    targets = ([(ups[k], 1 - x) for k in mates] + [(y, 1 - x)] + [(ups[k], x) for k in mates]
               + [(y, x)])
    at_x, at_y, at_me = tall - 1, tall, chips - 1
    sib, via_x, via_y = [], [], []
    in_x, in_y = [None, None], [[None, None] for _ in mates]

    def finish(s, part):
        sib[s].wait_recv()
        e_sum[s] = (part + e_sib[s].astype(F32)).astype(BF16)
        low, high = e_sum.at[s, :mid], e_sum.at[s, mid:]
        if s < at_x:
            via_x.append(post(low, e_via_x.at[s], evx_send.at[s], evx_recv.at[s],
                              {"loop": across}))
            via_y.append(post(high, e_via_y.at[s], evy_send.at[s], evy_recv.at[s],
                              {"loop": device(ups[s], x, par)}))
        elif s == at_x:
            in_x[0] = post(low, e_x.at[0], ex_send.at[0], ex_recv.at[0], {"loop": across})
        elif s < at_me:
            k = s - at_y
            in_y[k][1] = post(high, e_y.at[k, 1], ey_send.at[k, 1], ey_recv.at[k, 1],
                              {"loop": device(ups[k], x, par)})

    def offer(s, src):
        sib.append(post(src, e_sib.at[s], es_send.at[s], es_recv.at[s], {"loop": sibling}))

    if chunk % LANES == 0:
        def sums(s, which):
            picked = [rows[:, pl.ds(pl.multiple_of(((yy * 2 + xx) * 2 + which) * chunk, chunk), chunk)]
                      for yy, xx in targets[s:s + 2]]
            part = dot(grads[...], jnp.concatenate(picked, axis=1))
            return part[:, :chunk], part[:, chunk:]

        for s in range(0, chips, 2):
            for j, part in enumerate(sums(s, 1 - par)):
                e_own[s + j, 0] = part.astype(BF16)
                offer(s + j, e_own.at[s + j, 0])
        for s in range(0, chips, 2):
            for j, part in enumerate(sums(s, par)):
                finish(s + j, part)
    else:
        for s, (yy, xx) in enumerate(targets):
            cols = pl.ds(pl.multiple_of((yy * 2 + xx) * 2 * chunk, 2 * chunk), 2 * chunk)
            part = dot(grads[...], rows[:, cols]).astype(BF16)
            e_own[s, 0] = part[:, :chunk]
            e_own[s, 1] = part[:, chunk:]
            offer(s, e_own.at[s, 1 - par])
        for s in range(chips):
            finish(s, e_own[s, par].astype(F32))

    permutation(ctx, per)

    for k in mates:
        via_x[k].wait_recv()
        total = e_sum[at_y + k, :mid].astype(F32) + e_via_x[k].astype(F32)
        e_fwd_y[k] = total.astype(BF16)
        in_y[k][0] = post(e_fwd_y.at[k], e_y.at[k, 0], ey_send.at[k, 0], ey_recv.at[k, 0],
                          {"loop": device(ups[k], x, par)})
    total = e_sum[at_x, mid:].astype(F32)
    for k in mates:
        via_y[k].wait_recv()
        total = total + e_via_y[k].astype(F32)
    e_fwd_x[...] = total.astype(BF16)
    in_x[1] = post(e_fwd_x, e_x.at[1], ex_send.at[1], ex_recv.at[1], {"loop": across})

    for k in range(chips - 1):
        far[k].wait_recv()
        src = held.at[(chip + chips - 1 - k) % chips * 2 + par]
        near.append(post(src, src, hs_send.at[k], hs_recv.at[k], {"loop": sibling}))

    @pl.loop(0, cands // TILE)
    def _(t):
        cols = pl.ds(pl.multiple_of(t * TILE, TILE), TILE)
        gradt[:, cols] = lax.dot_general(
            perm[...], grads[cols, :], NT, preferred_element_type=F32).astype(BF16)

    for copy in near:
        copy.wait_recv()
    hid_all = held.reshape(cands, width)

    @pl.loop(0, width // LANES)
    def _(t):
        cols = pl.ds(pl.multiple_of(t * LANES, LANES), LANES)
        hidt[cols, :] = hid_all[:, cols].T

    halves = []
    for h in range(2):
        total = e_sum[at_me, h * mid:(h + 1) * mid].astype(F32)
        in_x[h].wait_recv()
        total = total + e_x[h].astype(F32)
        for k in mates:
            in_y[k][h].wait_recv()
            total = total + e_y[k, h].astype(F32)
        halves.append(total.astype(BF16))
    e_all = jnp.concatenate(halves, axis=0)
    out_rows = proj_out.shape[0]
    pl.semaphore_wait(ready, ring - 1)

    def outgoing(k):
        to, there = (me + k % ring) % ring, (group + k // ring) % groups
        return pltpu.make_async_remote_copy(
            src_ref=p_own.at[there, to], dst_ref=p_in.at[k], send_sem=p_send.at[k],
            recv_sem=p_recv.at[k], device_id={"loop": to, "dp": there}, device_id_type=MESH)

    quarter = ring // 4
    for t in range(4):
        places = [(me + t * quarter + j) % ring for j in range(quarter)]
        lines = groups * out_rows
        strip = dot(jnp.concatenate(
            [hidt[pl.ds(pl.multiple_of(l * lines, lines), lines), :] for l in places], axis=0), e_all)
        for j, l in enumerate(places):
            for g in range(groups):
                first = j * lines + g * out_rows
                p_own[g, l] = strip[first:first + out_rows].astype(BF16)
        for j in range(quarter):
            outgoing(ring + t * quarter + j).start()

    @pl.loop(2 * ring, groups * ring)
    def _(k):
        outgoing(k).start()

    @pl.loop(1, ring)
    def _(k):
        outgoing(k).start()

    @pl.loop(0, n_rows // TILE)
    def _(t):
        at = pl.ds(pl.multiple_of(t * TILE, TILE), TILE)
        code_ref[at, :] = dot(gradt[at, :], embed[...])

    p_in[0] = p_own[group, me]

    @pl.loop(1, ring * groups)
    def _(k):
        outgoing(k).wait_recv()

    for l in range(ring):
        slot = (me + ring - l) % ring
        total = p_in[slot].astype(F32)
        for g in range(1, groups):
            total = total + p_in[g * ring + slot].astype(F32)
        proj_out[:, l * chunk:(l + 1) * chunk] = total

    @pl.loop(1, ring * groups)
    def _(k):
        outgoing(k).wait_send()

    for copy in started:
        copy.wait_send()


def write_body(code_ref, loss_ref, proj_ref, code_out, loss_out, proj_out, sems):
    parts = sems.shape[0] - 2
    step = code_ref.shape[0] // parts
    copies = [
        pltpu.make_async_copy(code_ref.at[pl.ds(i * step, step)], code_out.at[pl.ds(i * step, step)],
                              sems.at[i])
        for i in range(parts)
    ]
    copies.append(pltpu.make_async_copy(proj_ref, proj_out, sems.at[parts]))
    copies.append(pltpu.make_async_copy(loss_ref, loss_out, sems.at[parts + 1]))
    for copy in copies:
        copy.start()
    for copy in copies:
        copy.wait()


def local(ring, groups, codes, cand_hidden, proj, gold):
    ctx, per, width = codes.shape
    batch = cand_hidden.shape[0]
    n_rows = ctx * per
    chips = ring // 2
    mates = chips // 2 - 1
    cands = ring * batch
    out_rows = width // (ring * groups)
    chunk = width // ring
    vmem = pl.BlockSpec(memory_space=pltpu.VMEM)
    hbm = pl.BlockSpec(memory_space=pltpu.HBM)
    dma = pltpu.SemaphoreType.DMA
    results = (
        jax.ShapeDtypeStruct((1, ctx), F32),
        jax.ShapeDtypeStruct((n_rows, width), F32),
        jax.ShapeDtypeStruct((out_rows, width), F32),
    )
    inputs = [pltpu.with_memory_space_constraint(v, pltpu.HBM) for v in (
        codes.reshape(n_rows, width), cand_hidden, proj, gold.reshape(1, ctx))]
    loss, code_grad, proj_grad = pl.pallas_call(
        functools.partial(body, ring, groups, ctx, per),
        name="link_step",
        out_shape=results,
        in_specs=[hbm, hbm, hbm, hbm],
        out_specs=(vmem, vmem, vmem),
        scratch_shapes=[
            pltpu.VMEM((n_rows, width), BF16),
            pltpu.VMEM((width, width), BF16),
            pltpu.VMEM((1, ctx), jnp.int32),
            pltpu.VMEM((n_rows, n_rows), BF16),
            pltpu.VMEM((n_rows, width), BF16),
            pltpu.VMEM((ring, batch, width), BF16),
            pltpu.VMEM((cands, width), BF16),
            pltpu.VMEM((2, chips * batch, n_rows), F32),
            pltpu.VMEM((cands, n_rows), F32),
            pltpu.VMEM((cands, LANES), F32),
            pltpu.VMEM((cands, n_rows), BF16),
            pltpu.VMEM((n_rows, cands), BF16),
            pltpu.VMEM((width, cands), BF16),
            pltpu.VMEM((chips, 2, cands, chunk), BF16),
            pltpu.VMEM((chips, cands, chunk), BF16),
            pltpu.VMEM((chips, cands, chunk), BF16),
            pltpu.VMEM((mates, cands // 2, chunk), BF16),
            pltpu.VMEM((mates, cands // 2, chunk), BF16),
            pltpu.VMEM((2, cands // 2, chunk), BF16),
            pltpu.VMEM((mates, 2, cands // 2, chunk), BF16),
            pltpu.VMEM((cands // 2, chunk), BF16),
            pltpu.VMEM((mates, cands // 2, chunk), BF16),
            pltpu.VMEM((groups, ring, out_rows, chunk), BF16),
            pltpu.VMEM((groups * ring, out_rows, chunk), BF16),
            dma((3,)), dma((width // TILE,)),
            dma((2,)), dma((2,)), dma((mates, 2)), dma((mates, 2)),
            dma((mates,)), dma((mates,)), dma((mates,)), dma((mates,)),
            dma((chips,)), dma((chips,)),
            dma((chips - 1,)), dma((chips - 1,)), dma((chips,)), dma((chips,)),
            dma((chips,)), dma((chips,)),
            dma((mates,)), dma((mates,)), dma((mates,)), dma((mates,)),
            dma((2,)), dma((2,)), dma((mates, 2)), dma((mates, 2)),
            dma((groups * ring,)), dma((groups * ring,)), pltpu.SemaphoreType.REGULAR,
        ],
        compiler_params=pltpu.CompilerParams(
            collective_id=0, has_side_effects=True, vmem_limit_bytes=44 * 2**20),
    )(*inputs)
    code_grad, loss, proj_grad = pl.pallas_call(
        write_body,
        name="code_grad",
        out_shape=(results[1], results[0], results[2]),
        in_specs=[vmem, vmem, vmem],
        out_specs=(pl.BlockSpec(memory_space=pl.ANY),) * 3,
        scratch_shapes=[dma((8 + 2,))],
        compiler_params=pltpu.CompilerParams(vmem_limit_bytes=8 * 2**20),
    )(code_grad, loss, proj_grad)
    return loss.reshape(ctx), code_grad.reshape(ctx, per, width), proj_grad


def solution(mesh):
    return jax.shard_map(
        functools.partial(local, mesh.shape["loop"], mesh.shape["dp"]),
        mesh=mesh,
        in_specs=(P(("loop", "dp"), None, None), P(("loop", "dp"), None), P(), P(("loop", "dp"))),
        out_specs=(P(("loop", "dp")), P(("loop", "dp"), None, None), P(("loop", "dp"), None)),
        check_vma=False,
    )
```
